32 devices in a mesh: groups: 2 (over y), expert: 4 (over z), dp: 2 (over x), mp: 2 (over core).
Axes of the slice: x: 2, y: 2, z: 4, core: 2. Of those that a mesh axis runs over, the one named last changes fastest.
Arguments:
- latent: float32 [512, 2048], P(('groups', 'expert', 'dp', 'mp')), parts along dimension 0, may hold values from -6 to 6
- time_embedding: float32 [2048], replicated, may hold values from -6 to 6
- norm_gain: float32 [2, 2048], replicated, may hold values from 0.1 to 1.9
- router: float32 [2, 2048, 16], replicated, may hold values from -0.03125 to 0.03125
- up_proj: bfloat16 [2, 16, 2048, 1408], P(None, 'expert', None, 'dp'), may hold values from -0.125 to 0.125
- down_proj: bfloat16 [2, 16, 1408, 2048], P(None, 'expert', 'dp'), may hold values from -0.15625 to 0.15625
- routes: int32 [2, 2, 512, 2], P(None, None, ('groups', 'expert', 'dp', 'mp')), parts along dimension 2, may hold values from 0 to 15, all different within a row; in each aligned block of 16 rows (0 to 15, 16 to 31, ..., all dimensions but the last counted through in order) at most 2 rows name the same one
Outputs:
- next_latent: float32 [512, 2048], P(('groups', 'expert', 'dp', 'mp')), parts along dimension 0
- mean_velocity: float32 [512, 2048], P(('groups', 'expert', 'dp', 'mp')), parts along dimension 0
The draws below stay inside these ranges and needn't reach their ends.
There are 2 independent parts, one for each index of `groups`. The reference program is written for one: setup_inputs(seed, part) draws one part's arguments, and reference() takes and returns one part's arrays. A program takes and returns all parts, laid end to end along the dimension named above; an argument that names none is the same for every part. Nothing has to cross between parts.
Inputs may be any that keep to these rules, and one draw needn't show every extreme that they name: `routes`: in each evaluation and layer, the 16 tokens of one device (aligned blocks along the token dimension) name any one expert at most 2 times, a bound that some block reaches by one device's tokens; a token's two experts differ.
All inputs are finite; a program needn't handle non-finite values.
Results may differ from the reference program's by a relative error of at most 0.0055.
Values may be sent and summed in bfloat16 or wider, within the bound.
No kernel may reach another device: no remote copies, remote signals or barrier semaphores. Data moves between devices by JAX's collectives and lax.ppermute only.
A program may use at most 128 MiB of HBM per device.

```python
import math
import jax
import jax.numpy as jnp
import numpy as np
from jax import lax

D = 2048
FF = 1408
EXPERTS = 16
TOP = 2
LAYERS = 2
TOK_DEV = 16
CAP = 2
TOKENS = 256
N_DP = 2


def shard_levels(stream_key, dims, shards, low, largest):
    def one(dim, blocks):
        draws = jax.random.uniform(jax.random.fold_in(jax.random.fold_in(stream_key, 6), dim), (blocks,), jnp.float32, low / len(shards), largest / len(shards))
        return jnp.repeat(jnp.exp(draws), dims[dim] // blocks).reshape((-1,) + (1,) * (len(dims) - dim - 1))

    loudness = one(*shards[0])
    for cut in shards[1:]:
        loudness = loudness * one(*cut)
    return loudness


def shared_out(stream_key, own, number, rows, amount, top, most, slope):
    sequence = jax.random.permutation(stream_key, amount)
    packed, ordinary = shares(amount, rows * top, most, slope, True), shares(amount, rows * top, most, slope, False)
    places = jnp.arange(amount)

    def named(sizes, turn):
        used = int((sizes > 0).sum())
        fixed = max(1, used // 4)
        moved = fixed + (places - fixed + turn * (used - fixed)) % max(1, amount - fixed)
        return jnp.zeros((amount,), jnp.int32).at[sequence[jnp.where(places < fixed, places, moved)]].set(jnp.asarray(sizes, jnp.int32))

    sizes = jnp.where(number % 4 == 0, named(packed, number // 4), named(ordinary, number - number // 4 - 1))
    mixed = jax.random.permutation(jax.random.fold_in(own, 3), amount)
    donor, receiver = mixed[0:amount // 2 * 2:2], mixed[1:amount // 2 * 2:2]
    room = jnp.minimum(sizes[donor] - 1, most - sizes[receiver]) // 2
    room = jnp.where((donor == sequence[0]) | (receiver == sequence[0]) | (sizes[receiver] == 0), 0, jnp.maximum(room, 0))
    moved = jax.random.randint(jax.random.fold_in(own, 4), (amount // 2,), 0, 1 << 20) % (room + 1)
    sizes = sizes.at[donor].add(-moved).at[receiver].add(moved)
    labels = jnp.searchsorted(jnp.cumsum(sizes), jnp.arange(rows * top), side="right").astype(jnp.int32)
    listing = labels.reshape(top, rows).T
    listing = listing[jax.random.permutation(jax.random.fold_in(own, 1), rows)]
    turn = jax.random.randint(jax.random.fold_in(own, 2), (rows, 1), 0, top)
    return jnp.take_along_axis(listing, (jnp.arange(top)[None, :] + turn) % top, axis=1)


def shares(count, total, limit, skew, full):
    portions = [(1 << 20) // math.isqrt(rank ** skew) + 1 for rank in range(1, count + 1)]
    largest = limit if full else min(limit, max(-(-total // count), total * portions[0] // sum(portions)))
    least = 1 if total - largest >= count - 1 else 0
    given, rest = [largest] + [least] * (count - 1), total - largest - least * (count - 1)
    while rest > 0:
        free = [i for i in range(1, count) if given[i] < largest] or [i for i in range(1, count) if given[i] < limit]
        mass, left = sum([portions[i] for i in free]), rest
        for i in free:
            more = min(limit - given[i], max(1, left * portions[i] // mass), rest)
            given[i] = given[i] + more
            rest = rest - more
    return np.array(given)


def noise(rng, extent, width, most, split=(), held_as=jnp.bfloat16):
    result = jax.random.normal(rng, extent, jnp.float32) * width
    if len(split) > 0:
        result = shard_levels(rng, extent, split, -0.22, 0.18) * result
    return jnp.clip(result, min=-most, max=most).astype(held_as)


def setup_inputs(seed: int = 0, part: int = 0) -> dict:
    keys = jax.random.split(jax.random.key(seed), 8)
    part_keys = jax.random.split(jax.random.fold_in(keys[7], part), 8)
    latent = noise(part_keys[0], (TOKENS, D), 1.0, 6.0, ((0, 16),), jnp.float32)
    time_embedding = noise(keys[1], (D,), 1.0, 6.0, (), jnp.float32)
    norm_gain = jnp.clip(1.0 + 0.18 * jax.random.normal(keys[2], (LAYERS, D), jnp.float32), 0.1, 1.9)
    router = noise(keys[3], (LAYERS, D, EXPERTS), (16 * D) ** -0.5, 0.03125, (), jnp.float32)
    up_proj = noise(keys[4], (LAYERS, EXPERTS, D, FF), D ** -0.5, 0.125, ((1, 4), (3, 2)))
    down_proj = noise(keys[5], (LAYERS, EXPERTS, FF, D), FF ** -0.5, 0.15625, ((1, 4), (2, 2)))
    routes_keys = jax.random.split(jax.random.fold_in(part_keys[6], 1), 2 * LAYERS * TOKENS // TOK_DEV)
    routes_turns = jax.random.permutation(jax.random.fold_in(part_keys[6], 3), 2 * LAYERS * TOKENS // TOK_DEV)
    routes = jax.vmap(lambda own, number: shared_out(jax.random.fold_in(part_keys[6], 2), own, number, TOK_DEV, EXPERTS, TOP, CAP, 2))(routes_keys, routes_turns).reshape((2, LAYERS, TOKENS, TOP))
    return {"latent": latent, "time_embedding": time_embedding, "norm_gain": norm_gain, "router": router, "up_proj": up_proj, "down_proj": down_proj, "routes": routes}


epsilon = 1e-06
start_time = 1.0
step_size = -0.5

def mix_weights(scaled, router_layer, chosen):
    logits = jnp.dot(scaled, router_layer, precision=lax.Precision.HIGHEST)
    picked = jnp.take_along_axis(logits, chosen, axis=1)
    leading = jax.nn.sigmoid(picked[:, 0] - picked[:, 1])
    return jnp.stack([leading, 1.0 - leading], axis=1)

def expert_layer(normed, chosen, up_layer, down_layer):
    blocks = TOKENS // TOK_DEV
    row_count = TOK_DEV * TOP
    flat_choice = chosen.reshape(blocks, row_count).astype(jnp.int32)
    onehot = (flat_choice[:, :, None] == jnp.arange(EXPERTS, dtype=jnp.int32)[None, None, :]).astype(jnp.int32)
    before = jnp.cumsum(onehot, axis=1) - onehot
    position = lax.optimization_barrier(jnp.sum(before * onehot, axis=2)).astype(jnp.int32)
    block_index = jnp.broadcast_to(jnp.arange(blocks, dtype=jnp.int32)[:, None], (blocks, row_count))
    token_index = (block_index * TOK_DEV + jnp.broadcast_to(jnp.arange(row_count, dtype=jnp.int32)[None, :] // TOP, (blocks, row_count))).astype(jnp.int32)
    slot_owner = jnp.full((EXPERTS, blocks, CAP), -1, dtype=jnp.int32)
    slot_owner = slot_owner.at[flat_choice, block_index, position].set(token_index)
    block_width = FF // N_DP

    def one_expert(expert_id):
        slot_index = slot_owner[expert_id].reshape(-1)
        slot_rows = jnp.where((slot_index >= 0)[:, None], normed[jnp.maximum(slot_index, 0)], jnp.zeros((), jnp.bfloat16))
        hidden = jax.nn.gelu(jnp.dot(slot_rows, up_layer[expert_id], preferred_element_type=jnp.float32), approximate=True).astype(jnp.bfloat16)
        summed = jnp.zeros((slot_rows.shape[0], D), jnp.float32)
        for block_number in range(N_DP):
            partial_value = jnp.dot(hidden[:, block_number * block_width:(block_number + 1) * block_width], down_layer[expert_id, block_number * block_width:(block_number + 1) * block_width], preferred_element_type=jnp.float32).astype(jnp.bfloat16)
            partial_value = lax.optimization_barrier(partial_value)
            summed = summed + partial_value.astype(jnp.float32)
        return summed.astype(jnp.bfloat16)
    outputs = lax.map(one_expert, jnp.arange(EXPERTS, dtype=jnp.int32))
    picked = outputs[flat_choice, (block_index * CAP + position).astype(jnp.int32)]
    return picked.reshape(TOKENS, TOP, D)

def moe_block(state, gain, router_layer, up_layer, down_layer, chosen):
    inverse = lax.rsqrt(lax.optimization_barrier(jnp.mean(state * state, axis=1, keepdims=True)) + epsilon)
    scaled = state * inverse * gain[None, :]
    normed = scaled.astype(jnp.bfloat16)
    weights = mix_weights(scaled, router_layer, chosen)
    picked = expert_layer(normed, chosen, up_layer, down_layer)
    return state + lax.optimization_barrier(jnp.sum(weights[:, :, None] * picked.astype(jnp.float32), axis=1))

def velocity(latent_now, time_now, section_routes, time_embedding, norm_gain, router, up_proj, down_proj):
    state = latent_now + time_now * time_embedding[None, :]
    for layer_index in range(LAYERS):
        state = moe_block(state, norm_gain[layer_index], router[layer_index], up_proj[layer_index], down_proj[layer_index], section_routes[layer_index])
    return state - latent_now

def reference(latent, time_embedding, norm_gain, router, up_proj, down_proj, routes):
    first = velocity(latent, start_time, routes[0], time_embedding, norm_gain, router, up_proj, down_proj)
    moved = latent + step_size * first
    second = velocity(moved, start_time + step_size, routes[1], time_embedding, norm_gain, router, up_proj, down_proj)
    mean_velocity = 0.5 * (first + second)
    return (latent + step_size * mean_velocity, mean_velocity)
```

```python
import math

import jax
import jax.numpy as jnp
from jax import lax
from jax.experimental import pallas as pl
from jax.experimental.pallas import tpu as pltpu
from jax.sharding import PartitionSpec as P

CAP = 2

epsilon = 1e-06
start_time = 1.0
step_size = -0.5

bf16 = jnp.bfloat16
f32 = jnp.float32
i32 = jnp.int32


def div(x, n):
    if n & (n - 1) == 0:
        return x >> (n.bit_length() - 1)
    return x // n


def rem(x, n):
    if n & (n - 1) == 0:
        return x & (n - 1)
    return x - (x // n) * n


class Plan:
    def __init__(self, mesh, tokens, width, experts, local_experts):
        n_mp = mesh.shape["mp"]
        self.share = n_mp if local_experts % n_mp == 0 else 1
        self.axes = ("expert", "dp", "mp") if self.share > 1 else ("expert", "dp")
        self.n_dp = mesh.shape["dp"]
        self.peers = mesh.shape["expert"] * self.n_dp * self.share
        self.tokens = tokens
        self.width = width
        self.experts = experts
        self.local_experts = local_experts
        self.mine = local_experts // self.share
        self.rows = self.mine * CAP
        self.parts = 8 // math.gcd(8, self.rows)
        self.piece = width // self.parts
        self.block = self.rows * self.parts
        self.total = self.peers * self.block

    def where(self, index):
        peer = div(index, self.block)
        inner = rem(index, self.block)
        part = div(inner, self.rows)
        row = rem(inner, self.rows)
        expert = div(peer, self.n_dp * self.share) * self.local_experts
        if self.share > 1:
            expert = expert + rem(peer, self.share) * self.mine
        return part, expert + div(row, CAP), rem(row, CAP)


def column(row, tokens):
    eye = lax.broadcasted_iota(i32, (tokens, tokens), 0) == lax.broadcasted_iota(
        i32, (tokens, tokens), 1
    )
    return jnp.sum(jnp.where(eye, row, 0), axis=1, keepdims=True)


def dispatch_select(plan, first, second):
    shape = (plan.total, plan.tokens)
    part, expert, slot = plan.where(lax.broadcasted_iota(i32, shape, 0))
    named = jnp.where((first == expert) | (second == expert), 1.0, 0.0)
    earlier = jnp.where(
        lax.broadcasted_iota(i32, (plan.tokens, plan.tokens), 0)
        < lax.broadcasted_iota(i32, (plan.tokens, plan.tokens), 1),
        1.0,
        0.0,
    ).astype(bf16)
    before = jnp.dot(named.astype(bf16), earlier, preferred_element_type=f32)
    chosen = jnp.where(before == slot.astype(f32), named, 0.0)
    return [jnp.where(part == p, chosen, 0.0).astype(bf16) for p in range(plan.parts)]


def combine_select(plan, first, second, mix):
    shape = (plan.tokens, plan.total)
    part, expert, slot = plan.where(lax.broadcasted_iota(i32, shape, 1))
    is_first = first == expert
    is_second = second == expert
    named = jnp.where(is_first | is_second, 1.0, 0.0)
    earlier = jnp.where(
        lax.broadcasted_iota(i32, (plan.tokens, plan.tokens), 1)
        < lax.broadcasted_iota(i32, (plan.tokens, plan.tokens), 0),
        1.0,
        0.0,
    ).astype(bf16)
    before = jnp.dot(earlier, named.astype(bf16), preferred_element_type=f32)
    weight = jnp.where(is_first, mix, 0.0) + jnp.where(is_second, 1.0 - mix, 0.0)
    return jnp.where(before == slot.astype(f32), weight, 0.0)


def combine(plan, state, weight, returned):
    part, _, _ = plan.where(lax.broadcasted_iota(i32, weight.shape, 1))
    high = weight.astype(bf16).astype(f32)
    middle = (weight - high).astype(bf16).astype(f32)
    low = weight - high - middle
    stacked = jnp.concatenate(
        [
            jnp.where(part == p, term, 0.0)
            for p in range(plan.parts)
            for term in (high, middle, low)
        ],
        axis=0,
    ).astype(bf16)
    product = jnp.dot(stacked, returned, preferred_element_type=f32)
    t = plan.tokens
    pieces = []
    for p in range(plan.parts):
        base = 3 * t * p
        pieces.append(
            product[base : base + t]
            + product[base + t : base + 2 * t]
            + product[base + 2 * t : base + 3 * t]
        )
    return state + jnp.concatenate(pieces, axis=1)


def emit_dispatch(plan, state, gain, router, routes, slots_ref, weight_ref):
    inverse = lax.rsqrt(jnp.mean(state * state, axis=1, keepdims=True) + epsilon)
    scaled = state * inverse * gain
    normed = scaled.astype(bf16)
    first = routes[0:1]
    second = routes[1:2]
    select = dispatch_select(plan, first, second)
    sent = jnp.zeros((plan.total, plan.piece), f32)
    for p in range(plan.parts):
        sent = sent + jnp.dot(
            select[p],
            normed[:, p * plan.piece : (p + 1) * plan.piece],
            preferred_element_type=f32,
        )
    slots_ref[...] = sent.astype(bf16)
    logits = lax.dot_general(
        scaled,
        router,
        (((1,), (1,)), ((), ())),
        precision=lax.Precision.HIGHEST,
        preferred_element_type=f32,
    )
    first_column = column(first, plan.tokens)
    second_column = column(second, plan.tokens)
    lane = lax.broadcasted_iota(i32, (plan.tokens, plan.experts), 1)
    gap = jnp.sum(
        jnp.where(lane == first_column, logits, 0.0)
        - jnp.where(lane == second_column, logits, 0.0),
        axis=1,
        keepdims=True,
    )
    mix = jax.nn.sigmoid(gap)
    weight_ref[...] = combine_select(plan, first_column, second_column, mix)


def per_device_fn(mesh):
    vmem = pl.BlockSpec(memory_space=pltpu.VMEM)

    def run(latent, time_embedding, norm_gain, router, up_proj, down_proj, routes):
        tokens, width = latent.shape
        layers, _, experts = router.shape
        local_experts = up_proj.shape[1]
        hidden = up_proj.shape[3]
        plan = Plan(mesh, tokens, width, experts, local_experts)
        mine = plan.mine

        embedding = time_embedding.reshape(1, width)
        router_t = jnp.swapaxes(router, 1, 2)
        routes_t = jnp.swapaxes(routes, 2, 3)

        def call(body, outs, args, **kw):
            return pl.pallas_call(
                body,
                out_shape=outs,
                in_specs=[vmem] * len(args),
                out_specs=[vmem] * len(outs),
                compiler_params=pltpu.CompilerParams(vmem_limit_bytes=16 << 20),
                **kw,
            )(*args)

        state_shape = jax.ShapeDtypeStruct((tokens, width), f32)
        slots_shape = pltpu.VMEM((plan.total, plan.piece), bf16)
        weight_shape = pltpu.VMEM((tokens, plan.total), f32)

        def begin(step, layer):
            def body(latent_ref, emb_ref, gain_ref, router_ref, routes_ref, state_ref, slots_ref, weight_ref):
                state = latent_ref[...] + start_time * emb_ref[...]
                state_ref[...] = state
                emit_dispatch(
                    plan, state, gain_ref[layer : layer + 1], router_ref[layer],
                    routes_ref[step, layer], slots_ref, weight_ref,
                )

            return call(
                body, [state_shape, slots_shape, weight_shape],
                [latent, embedding, norm_gain, router_t, routes_t],
            )

        def middle(step, layer, state, weight, returned):
            def body(state_in, weight_in, returned_ref, gain_ref, router_ref, routes_ref, state_ref, slots_ref, weight_ref):
                state = combine(plan, state_in[...], weight_in[...], returned_ref[...])
                state_ref[...] = state
                emit_dispatch(
                    plan, state, gain_ref[layer : layer + 1], router_ref[layer],
                    routes_ref[step, layer], slots_ref, weight_ref,
                )

            return call(
                body, [state_shape, slots_shape, weight_shape],
                [state, weight, returned, norm_gain, router_t, routes_t],
            )

        def turn(step, layer, state, weight, returned):
            def body(latent_ref, emb_ref, state_in, weight_in, returned_ref, gain_ref, router_ref, routes_ref,
                     first_ref, state_ref, slots_ref, weight_ref):
                state = combine(plan, state_in[...], weight_in[...], returned_ref[...])
                first = state - latent_ref[...]
                first_ref[...] = first
                moved = latent_ref[...] + step_size * first
                state = moved + (start_time + step_size) * emb_ref[...]
                state_ref[...] = state
                emit_dispatch(
                    plan, state, gain_ref[layer : layer + 1], router_ref[layer],
                    routes_ref[step, layer], slots_ref, weight_ref,
                )

            return call(
                body, [state_shape, state_shape, slots_shape, weight_shape],
                [latent, embedding, state, weight, returned, norm_gain, router_t, routes_t],
            )

        def finish(state, weight, returned, first):
            def body(latent_ref, state_in, weight_in, returned_ref, first_ref, next_ref, mean_ref):
                state = combine(plan, state_in[...], weight_in[...], returned_ref[...])
                first = first_ref[...]
                moved = latent_ref[...] + step_size * first
                mean = 0.5 * (first + (state - moved))
                mean_ref[...] = mean
                next_ref[...] = latent_ref[...] + step_size * mean

            return call(body, [state_shape, state_shape], [latent, state, weight, returned, first])

        def load(layer):
            def body(up_ref, down_ref, up_out, down_out, sems):
                base = lax.axis_index("mp") * mine if plan.share > 1 else 0
                a = pltpu.make_async_copy(up_ref.at[layer, pl.ds(base, mine)], up_out, sems.at[0])
                b = pltpu.make_async_copy(down_ref.at[layer, pl.ds(base, mine)], down_out, sems.at[1])
                a.start()
                b.start()
                a.wait()
                b.wait()

            return pl.pallas_call(
                body,
                out_shape=[
                    pltpu.VMEM((mine, width, hidden), bf16),
                    pltpu.VMEM((mine, hidden, width), bf16),
                ],
                in_specs=[pl.BlockSpec(memory_space=pl.ANY)] * 2,
                out_specs=[vmem] * 2,
                scratch_shapes=[pltpu.SemaphoreType.DMA((2,))],
                compiler_params=pltpu.CompilerParams(vmem_limit_bytes=2 << 20),
            )(up_proj, down_proj)

        each = plan.peers * CAP

        def experts_body(arrived_ref, up_ref, down_ref, out_ref):
            total = plan.rows * plan.peers

            def picks(shape, row_axis):
                row = lax.broadcasted_iota(i32, shape, row_axis)
                piece = lax.broadcasted_iota(i32, shape, 1 - row_axis)
                local = div(row, each)
                source = div(rem(row, each), CAP)
                target = source * plan.block + local * CAP + rem(row, CAP)
                return [
                    jnp.where(piece == target + p * plan.rows, 1.0, 0.0).astype(bf16)
                    for p in range(plan.parts)
                ]

            arrived = arrived_ref[...]
            rows = jnp.concatenate(
                [
                    jnp.dot(pick, arrived, preferred_element_type=f32).astype(bf16)
                    for pick in picks((total, plan.total), 0)
                ],
                axis=1,
            )
            results = []
            for local in range(mine):
                own = rows[local * each : (local + 1) * each]
                hid = jax.nn.gelu(
                    jnp.dot(own, up_ref[local], preferred_element_type=f32), approximate=True
                ).astype(bf16)
                results.append(jnp.dot(hid, down_ref[local], preferred_element_type=f32).astype(bf16))
            result = jnp.concatenate(results, axis=0)
            out = jnp.zeros((plan.total, plan.piece), f32)
            for p, pick in enumerate(picks((plan.total, total), 1)):
                out = out + jnp.dot(
                    pick, result[:, p * plan.piece : (p + 1) * plan.piece], preferred_element_type=f32
                )
            out_ref[...] = out.astype(bf16)

        def compute(arrived, layer_weights):
            return call(experts_body, [slots_shape], [arrived, *layer_weights])[0]

        def exchange(x):
            return lax.all_to_all(x, plan.axes, split_axis=0, concat_axis=0, tiled=True)

        state, slots, weight = begin(0, 0)
        loaded = [load(layer) for layer in range(layers)]
        first = None
        for step in range(2):
            for layer in range(layers):
                returned = exchange(compute(exchange(slots), loaded[layer]))
                if layer + 1 < layers:
                    state, slots, weight = middle(step, layer + 1, state, weight, returned)
                elif step == 0:
                    first, state, slots, weight = turn(1, 0, state, weight, returned)
                else:
                    return tuple(finish(state, weight, returned, first))

    return run


def solution(mesh):
    placed = (
        P(("groups", "expert", "dp", "mp"), None),
        P(),
        P(),
        P(),
        P(None, "expert", None, "dp"),
        P(None, "expert", "dp", None),
        P(None, None, ("groups", "expert", "dp", "mp"), None),
    )
    return jax.shard_map(
        per_device_fn(mesh),
        mesh=mesh,
        in_specs=placed,
        out_specs=(
            P(("groups", "expert", "dp", "mp"), None),
            P(("groups", "expert", "dp", "mp"), None),
        ),
        check_vma=False,
    )
```

```python
import math

import jax
import jax.numpy as jnp
from jax import lax
from jax.experimental import pallas as pl
from jax.experimental.pallas import tpu as pltpu
from jax.sharding import PartitionSpec as P

CAP = 2

epsilon = 1e-06
start_time = 1.0
step_size = -0.5

bf16 = jnp.bfloat16
f32 = jnp.float32
i32 = jnp.int32


def div(x, n):
    if n & (n - 1) == 0:
        return x >> (n.bit_length() - 1)
    return x // n


def rem(x, n):
    if n & (n - 1) == 0:
        return x & (n - 1)
    return x - (x // n) * n


class Plan:
    def __init__(self, mesh, tokens, width, experts, local_experts):
        n_mp = mesh.shape["mp"]
        self.share = n_mp if local_experts % n_mp == 0 else 1
        self.axes = ("expert", "dp", "mp") if self.share > 1 else ("expert", "dp")
        self.n_dp = mesh.shape["dp"]
        self.peers = mesh.shape["expert"] * self.n_dp * self.share
        self.tokens = tokens
        self.width = width
        self.experts = experts
        self.local_experts = local_experts
        self.mine = local_experts // self.share
        self.rows = self.mine * CAP
        self.parts = 8 // math.gcd(8, self.rows)
        self.piece = width // self.parts
        self.block = self.rows * self.parts
        self.total = self.peers * self.block

    def where(self, index):
        peer = div(index, self.block)
        inner = rem(index, self.block)
        part = div(inner, self.rows)
        row = rem(inner, self.rows)
        expert = div(peer, self.n_dp * self.share) * self.local_experts
        if self.share > 1:
            expert = expert + rem(peer, self.share) * self.mine
        return part, expert + div(row, CAP), rem(row, CAP)


def column(row, tokens):
    eye = lax.broadcasted_iota(i32, (tokens, tokens), 0) == lax.broadcasted_iota(
        i32, (tokens, tokens), 1
    )
    return jnp.sum(jnp.where(eye, row, 0), axis=1, keepdims=True)


def dispatch_select(plan, first, second):
    shape = (plan.total, plan.tokens)
    part, expert, slot = plan.where(lax.broadcasted_iota(i32, shape, 0))
    named = jnp.where((first == expert) | (second == expert), 1.0, 0.0)
    earlier = jnp.where(
        lax.broadcasted_iota(i32, (plan.tokens, plan.tokens), 0)
        < lax.broadcasted_iota(i32, (plan.tokens, plan.tokens), 1),
        1.0,
        0.0,
    ).astype(bf16)
    before = jnp.dot(named.astype(bf16), earlier, preferred_element_type=f32)
    chosen = jnp.where(before == slot.astype(f32), named, 0.0)
    return [jnp.where(part == p, chosen, 0.0).astype(bf16) for p in range(plan.parts)]


def combine_select(plan, first, second, mix):
    shape = (plan.tokens, plan.total)
    part, expert, slot = plan.where(lax.broadcasted_iota(i32, shape, 1))
    is_first = first == expert
    is_second = second == expert
    named = jnp.where(is_first | is_second, 1.0, 0.0)
    earlier = jnp.where(
        lax.broadcasted_iota(i32, (plan.tokens, plan.tokens), 1)
        < lax.broadcasted_iota(i32, (plan.tokens, plan.tokens), 0),
        1.0,
        0.0,
    ).astype(bf16)
    before = jnp.dot(earlier, named.astype(bf16), preferred_element_type=f32)
    weight = jnp.where(is_first, mix, 0.0) + jnp.where(is_second, 1.0 - mix, 0.0)
    return jnp.where(before == slot.astype(f32), weight, 0.0)


def combine(plan, state, weight, returned):
    part, _, _ = plan.where(lax.broadcasted_iota(i32, weight.shape, 1))
    high = weight.astype(bf16).astype(f32)
    middle = (weight - high).astype(bf16).astype(f32)
    low = weight - high - middle
    stacked = jnp.concatenate(
        [
            jnp.where(part == p, term, 0.0)
            for p in range(plan.parts)
            for term in (high, middle, low)
        ],
        axis=0,
    ).astype(bf16)
    product = jnp.dot(stacked, returned, preferred_element_type=f32)
    t = plan.tokens
    pieces = []
    for p in range(plan.parts):
        base = 3 * t * p
        pieces.append(
            product[base : base + t]
            + product[base + t : base + 2 * t]
            + product[base + 2 * t : base + 3 * t]
        )
    return state + jnp.concatenate(pieces, axis=1)


def emit_dispatch(plan, state, gain, router, routes, slots_ref, weight_ref):
    inverse = lax.rsqrt(jnp.mean(state * state, axis=1, keepdims=True) + epsilon)
    scaled = state * inverse * gain
    normed = scaled.astype(bf16)
    first = routes[0:1]
    second = routes[1:2]
    select = dispatch_select(plan, first, second)
    sent = jnp.zeros((plan.total, plan.piece), f32)
    for p in range(plan.parts):
        sent = sent + jnp.dot(
            select[p],
            normed[:, p * plan.piece : (p + 1) * plan.piece],
            preferred_element_type=f32,
        )
    slots_ref[...] = sent.astype(bf16)
    logits = lax.dot_general(
        scaled,
        router,
        (((1,), (1,)), ((), ())),
        precision=lax.Precision.HIGHEST,
        preferred_element_type=f32,
    )
    first_column = column(first, plan.tokens)
    second_column = column(second, plan.tokens)
    lane = lax.broadcasted_iota(i32, (plan.tokens, plan.experts), 1)
    gap = jnp.sum(
        jnp.where(lane == first_column, logits, 0.0)
        - jnp.where(lane == second_column, logits, 0.0),
        axis=1,
        keepdims=True,
    )
    mix = jax.nn.sigmoid(gap)
    weight_ref[...] = combine_select(plan, first_column, second_column, mix)


def per_device_fn(mesh):
    vmem = pl.BlockSpec(memory_space=pltpu.VMEM)
    hbm = pl.BlockSpec(memory_space=pltpu.HBM)

    def call(body, args, outs, copies=0, limit=8):
        return pl.pallas_call(
            body,
            out_shape=outs,
            in_specs=[spec for spec, _ in args],
            out_specs=[vmem] * len(outs),
            scratch_shapes=[pltpu.SemaphoreType.DMA((copies,))] if copies else [],
            compiler_params=pltpu.CompilerParams(vmem_limit_bytes=limit << 20),
        )(*[arg for _, arg in args])

    def here(*arrays):
        return [(vmem, x) for x in arrays]

    def far(*arrays):
        return [(hbm, pltpu.with_memory_space_constraint(x, pltpu.HBM)) for x in arrays]

    def run(latent, time_embedding, norm_gain, router, up_proj, down_proj, routes):
        tokens, width = latent.shape
        layers, _, experts = router.shape
        local_experts = up_proj.shape[1]
        hidden = up_proj.shape[3]
        plan = Plan(mesh, tokens, width, experts, local_experts)
        mine = plan.mine

        embedding = time_embedding.reshape(1, width)
        router_t = jnp.swapaxes(router, 1, 2)
        routes_t = jnp.swapaxes(routes, 2, 3)
        up_t = jnp.swapaxes(up_proj, 2, 3)

        out_shape = jax.ShapeDtypeStruct((tokens, width), f32)
        state_shape = pltpu.VMEM((tokens, width), f32)
        slots_shape = pltpu.VMEM((plan.total, plan.piece), bf16)
        weight_shape = pltpu.VMEM((tokens, plan.total), f32)
        up_shape = pltpu.VMEM((mine, hidden, width), bf16)

        def own_experts(ref, layer):
            base = lax.axis_index("mp") * mine if plan.share > 1 else 0
            return ref.at[layer, pl.ds(base, mine)]

        def begin():
            inputs = [latent, embedding, norm_gain, router_t, routes_t]
            count = len(inputs)

            def body(*refs):
                sources, (up_hbm,) = refs[:count], refs[count : count + 1]
                copies = refs[count + 1 : 2 * count + 1]
                state_ref, slots_ref, weight_ref, up_ref, sems = refs[2 * count + 1 :]
                moves = [
                    pltpu.make_async_copy(source, target, sems.at[i])
                    for i, (source, target) in enumerate(zip(sources, copies))
                ]
                moves.append(pltpu.make_async_copy(own_experts(up_hbm, 0), up_ref, sems.at[count]))
                for move in moves:
                    move.start()
                for move in moves[:count]:
                    move.wait()
                latent_ref, emb_ref, gain_ref, router_ref, routes_ref = copies
                state = latent_ref[...] + start_time * emb_ref[...]
                state_ref[...] = state
                emit_dispatch(
                    plan, state, gain_ref[0:1], router_ref[0], routes_ref[0, 0], slots_ref, weight_ref
                )
                moves[count].wait()

            outs = call(
                body,
                far(*inputs, up_t),
                [pltpu.VMEM(x.shape, x.dtype) for x in inputs]
                + [state_shape, slots_shape, weight_shape, up_shape],
                copies=count + 1,
            )
            return outs[:count], outs[count:]

        def middle(small, step, layer, state, weight, returned, loading):
            _, _, gain, router_s, routes_s = small

            def body(state_in, weight_in, returned_ref, gain_ref, router_ref, routes_ref, *refs):
                if loading:
                    up_hbm, state_ref, slots_ref, weight_ref, up_ref, sems = refs
                    move = pltpu.make_async_copy(own_experts(up_hbm, layer), up_ref, sems.at[0])
                    move.start()
                else:
                    state_ref, slots_ref, weight_ref = refs
                state = combine(plan, state_in[...], weight_in[...], returned_ref[...])
                state_ref[...] = state
                emit_dispatch(
                    plan, state, gain_ref[layer : layer + 1], router_ref[layer],
                    routes_ref[step, layer], slots_ref, weight_ref,
                )
                if loading:
                    move.wait()

            return call(
                body,
                here(state, weight, returned, gain, router_s, routes_s) + (far(up_t) if loading else []),
                [state_shape, slots_shape, weight_shape] + ([up_shape] if loading else []),
                copies=int(loading),
            )

        def turn(small, state, weight, returned):
            def body(latent_ref, emb_ref, gain_ref, router_ref, routes_ref, state_in, weight_in, returned_ref,
                     first_ref, state_ref, slots_ref, weight_ref):
                state = combine(plan, state_in[...], weight_in[...], returned_ref[...])
                first = state - latent_ref[...]
                first_ref[...] = first
                moved = latent_ref[...] + step_size * first
                state = moved + (start_time + step_size) * emb_ref[...]
                state_ref[...] = state
                emit_dispatch(
                    plan, state, gain_ref[0:1], router_ref[0], routes_ref[1, 0], slots_ref, weight_ref
                )

            return call(
                body, here(*small, state, weight, returned),
                [state_shape, state_shape, slots_shape, weight_shape],
            )

        def finish(small, state, weight, returned, first):
            def body(latent_ref, state_in, weight_in, returned_ref, first_ref, next_ref, mean_ref):
                state = combine(plan, state_in[...], weight_in[...], returned_ref[...])
                first = first_ref[...]
                moved = latent_ref[...] + step_size * first
                mean = 0.5 * (first + (state - moved))
                mean_ref[...] = mean
                next_ref[...] = latent_ref[...] + step_size * mean

            return call(body, here(small[0], state, weight, returned, first), [out_shape, out_shape])

        each = plan.peers * CAP

        def compute(arrived, up, down, layer):
            loading = down is None

            def body(arrived_ref, up_ref, down_in, out_ref, *refs):
                if loading:
                    down_ref, sems = refs
                    move = pltpu.make_async_copy(own_experts(down_in, layer), down_ref, sems.at[0])
                    move.start()
                else:
                    down_ref = down_in
                total = plan.rows * plan.peers

                def picks(shape, row_axis):
                    row = lax.broadcasted_iota(i32, shape, row_axis)
                    piece = lax.broadcasted_iota(i32, shape, 1 - row_axis)
                    local = div(row, each)
                    source = div(rem(row, each), CAP)
                    target = source * plan.block + local * CAP + rem(row, CAP)
                    return [
                        jnp.where(piece == target + p * plan.rows, 1.0, 0.0).astype(bf16)
                        for p in range(plan.parts)
                    ]

                arrived = arrived_ref[...]
                rows = jnp.concatenate(
                    [
                        jnp.dot(pick, arrived, preferred_element_type=f32).astype(bf16)
                        for pick in picks((total, plan.total), 0)
                    ],
                    axis=1,
                )
                hids = [
                    jax.nn.gelu(
                        lax.dot_general(
                            rows[local * each : (local + 1) * each],
                            up_ref[local],
                            (((1,), (1,)), ((), ())),
                            preferred_element_type=f32,
                        ),
                        approximate=True,
                    ).astype(bf16)
                    for local in range(mine)
                ]
                if loading:
                    move.wait()
                result = jnp.concatenate(
                    [
                        jnp.dot(hids[local], down_ref[local], preferred_element_type=f32).astype(bf16)
                        for local in range(mine)
                    ],
                    axis=0,
                )
                out = jnp.zeros((plan.total, plan.piece), f32)
                for p, pick in enumerate(picks((plan.total, total), 1)):
                    out = out + jnp.dot(
                        pick, result[:, p * plan.piece : (p + 1) * plan.piece], preferred_element_type=f32
                    )
                out_ref[...] = out.astype(bf16)

            down_args = far(down_proj) if loading else here(down)
            outs = call(
                body,
                here(arrived, up) + down_args,
                [slots_shape] + ([pltpu.VMEM((mine, hidden, width), bf16)] if loading else []),
                copies=int(loading),
                limit=16,
            )
            return outs[0], (outs[1] if loading else down)

        def exchange(x):
            return lax.all_to_all(x, plan.axes, split_axis=0, concat_axis=0, tiled=True)

        small, (state, slots, weight, up) = begin()
        ups, downs, first = [up], [], None
        for step in range(2):
            for layer in range(layers):
                result, down = compute(
                    exchange(slots), ups[layer], downs[layer] if step else None, layer
                )
                downs.append(down)
                returned = exchange(result)
                if layer + 1 < layers:
                    state, slots, weight, *loaded = middle(
                        small, step, layer + 1, state, weight, returned, step == 0
                    )
                    ups.extend(loaded)
                elif step == 0:
                    first, state, slots, weight = turn(small, state, weight, returned)
                else:
                    return tuple(finish(small, state, weight, returned, first))

    return run


def solution(mesh):
    placed = (
        P(("groups", "expert", "dp", "mp"), None),
        P(),
        P(),
        P(),
        P(None, "expert", None, "dp"),
        P(None, "expert", "dp", None),
        P(None, None, ("groups", "expert", "dp", "mp"), None),
    )
    return jax.shard_map(
        per_device_fn(mesh),
        mesh=mesh,
        in_specs=placed,
        out_specs=(
            P(("groups", "expert", "dp", "mp"), None),
            P(("groups", "expert", "dp", "mp"), None),
        ),
        check_vma=False,
    )
```

```python
import math

import jax
import jax.numpy as jnp
from jax import lax
from jax.experimental import pallas as pl
from jax.experimental.pallas import tpu as pltpu
from jax.sharding import PartitionSpec as P

CAP = 2

epsilon = 1e-06
start_time = 1.0
step_size = -0.5

bf16 = jnp.bfloat16
f32 = jnp.float32
i32 = jnp.int32


def div(x, n):
    if n & (n - 1) == 0:
        return x >> (n.bit_length() - 1)
    return x // n


def rem(x, n):
    if n & (n - 1) == 0:
        return x & (n - 1)
    return x - (x // n) * n


class Plan:
    def __init__(self, mesh, tokens, width, experts, local_experts):
        n_mp = mesh.shape["mp"]
        self.share = n_mp if local_experts % n_mp == 0 else 1
        self.axes = ("expert", "dp", "mp") if self.share > 1 else ("expert", "dp")
        self.n_dp = mesh.shape["dp"]
        self.peers = mesh.shape["expert"] * self.n_dp * self.share
        self.tokens = tokens
        self.width = width
        self.experts = experts
        self.local_experts = local_experts
        self.mine = local_experts // self.share
        self.rows = self.mine * CAP
        self.parts = 8 // math.gcd(8, self.rows)
        self.piece = width // self.parts
        self.block = self.rows * self.parts
        self.total = self.peers * self.block

    def where(self, index):
        peer = div(index, self.block)
        inner = rem(index, self.block)
        part = div(inner, self.rows)
        row = rem(inner, self.rows)
        expert = div(peer, self.n_dp * self.share) * self.local_experts
        if self.share > 1:
            expert = expert + rem(peer, self.share) * self.mine
        return part, expert + div(row, CAP), rem(row, CAP)


def column(row, tokens):
    eye = lax.broadcasted_iota(i32, (tokens, tokens), 0) == lax.broadcasted_iota(
        i32, (tokens, tokens), 1
    )
    return jnp.sum(jnp.where(eye, row, 0), axis=1, keepdims=True)


def dispatch_select(plan, first, second):
    shape = (plan.total, plan.tokens)
    part, expert, slot = plan.where(lax.broadcasted_iota(i32, shape, 0))
    named = jnp.where((first == expert) | (second == expert), 1.0, 0.0)
    earlier = jnp.where(
        lax.broadcasted_iota(i32, (plan.tokens, plan.tokens), 0)
        < lax.broadcasted_iota(i32, (plan.tokens, plan.tokens), 1),
        1.0,
        0.0,
    ).astype(bf16)
    before = jnp.dot(named.astype(bf16), earlier, preferred_element_type=f32)
    chosen = jnp.where(before == slot.astype(f32), named, 0.0)
    return [jnp.where(part == p, chosen, 0.0).astype(bf16) for p in range(plan.parts)]


def combine_select(plan, first, second, mix):
    shape = (plan.tokens, plan.total)
    part, expert, slot = plan.where(lax.broadcasted_iota(i32, shape, 1))
    is_first = first == expert
    is_second = second == expert
    named = jnp.where(is_first | is_second, 1.0, 0.0)
    earlier = jnp.where(
        lax.broadcasted_iota(i32, (plan.tokens, plan.tokens), 1)
        < lax.broadcasted_iota(i32, (plan.tokens, plan.tokens), 0),
        1.0,
        0.0,
    ).astype(bf16)
    before = jnp.dot(earlier, named.astype(bf16), preferred_element_type=f32)
    weight = jnp.where(is_first, mix, 0.0) + jnp.where(is_second, 1.0 - mix, 0.0)
    return jnp.where(before == slot.astype(f32), weight, 0.0)


def combine(plan, state, weight, returned):
    part, _, _ = plan.where(lax.broadcasted_iota(i32, weight.shape, 1))
    high = weight.astype(bf16).astype(f32)
    middle = (weight - high).astype(bf16).astype(f32)
    low = weight - high - middle
    stacked = jnp.concatenate(
        [
            jnp.where(part == p, term, 0.0)
            for p in range(plan.parts)
            for term in (high, middle, low)
        ],
        axis=0,
    ).astype(bf16)
    product = jnp.dot(stacked, returned, preferred_element_type=f32)
    t = plan.tokens
    pieces = []
    for p in range(plan.parts):
        base = 3 * t * p
        pieces.append(
            product[base : base + t]
            + product[base + t : base + 2 * t]
            + product[base + 2 * t : base + 3 * t]
        )
    return state + jnp.concatenate(pieces, axis=1)


def emit_dispatch(plan, state, gain, router, routes, slots_ref, weight_ref):
    inverse = lax.rsqrt(jnp.mean(state * state, axis=1, keepdims=True) + epsilon)
    scaled = state * inverse * gain
    normed = scaled.astype(bf16)
    first = routes[0:1]
    second = routes[1:2]
    select = dispatch_select(plan, first, second)
    sent = jnp.zeros((plan.total, plan.piece), f32)
    for p in range(plan.parts):
        sent = sent + jnp.dot(
            select[p],
            normed[:, p * plan.piece : (p + 1) * plan.piece],
            preferred_element_type=f32,
        )
    slots_ref[...] = sent.astype(bf16)
    logits = lax.dot_general(
        scaled,
        router,
        (((1,), (1,)), ((), ())),
        precision=lax.Precision.HIGHEST,
        preferred_element_type=f32,
    )
    first_column = column(first, plan.tokens)
    second_column = column(second, plan.tokens)
    lane = lax.broadcasted_iota(i32, (plan.tokens, plan.experts), 1)
    gap = jnp.sum(
        jnp.where(lane == first_column, logits, 0.0)
        - jnp.where(lane == second_column, logits, 0.0),
        axis=1,
        keepdims=True,
    )
    mix = jax.nn.sigmoid(gap)
    weight_ref[...] = combine_select(plan, first_column, second_column, mix)


def per_device_fn(mesh):
    vmem = pl.BlockSpec(memory_space=pltpu.VMEM)
    hbm = pl.BlockSpec(memory_space=pltpu.HBM)

    def call(body, args, outs, copies=0, limit=4):
        return pl.pallas_call(
            body,
            out_shape=outs,
            in_specs=[spec for spec, _ in args],
            out_specs=[vmem] * len(outs),
            scratch_shapes=[pltpu.SemaphoreType.DMA((copies,))] if copies else [],
            compiler_params=pltpu.CompilerParams(vmem_limit_bytes=limit << 20),
            cost_estimate=pl.CostEstimate(flops=10**11, transcendentals=0, bytes_accessed=10**9),
        )(*[arg for _, arg in args])

    def here(*arrays):
        return [(vmem, x) for x in arrays]

    def far(*arrays):
        return [(hbm, pltpu.with_memory_space_constraint(x, pltpu.HBM)) for x in arrays]

    def run(latent, time_embedding, norm_gain, router, up_proj, down_proj, routes):
        tokens, width = latent.shape
        layers, _, experts = router.shape
        local_experts = up_proj.shape[1]
        hidden = up_proj.shape[3]
        plan = Plan(mesh, tokens, width, experts, local_experts)
        mine = plan.mine

        embedding = time_embedding.reshape(1, width)
        router_t = jnp.swapaxes(router, 1, 2)
        routes_t = jnp.swapaxes(routes, 2, 3)
        up_t = jnp.swapaxes(up_proj, 2, 3)

        out_shape = jax.ShapeDtypeStruct((tokens, width), f32)
        state_shape = pltpu.VMEM((tokens, width), f32)
        slots_shape = pltpu.VMEM((plan.total, plan.piece), bf16)
        weight_shape = pltpu.VMEM((tokens, plan.total), f32)

        def begin():
            inputs = [latent, embedding, norm_gain, router_t, routes_t]
            count = len(inputs)

            def body(*refs):
                sources, copies = refs[:count], refs[count : 2 * count]
                state_ref, slots_ref, weight_ref, sems = refs[2 * count :]
                moves = [
                    pltpu.make_async_copy(source, target, sems.at[i])
                    for i, (source, target) in enumerate(zip(sources, copies))
                ]
                for move in moves:
                    move.start()
                for move in moves:
                    move.wait()
                latent_ref, emb_ref, gain_ref, router_ref, routes_ref = copies
                state = latent_ref[...] + start_time * emb_ref[...]
                state_ref[...] = state
                emit_dispatch(
                    plan, state, gain_ref[0:1], router_ref[0], routes_ref[0, 0], slots_ref, weight_ref
                )

            outs = call(
                body,
                far(*inputs),
                [pltpu.VMEM(x.shape, x.dtype) for x in inputs] + [state_shape, slots_shape, weight_shape],
                copies=count,
            )
            return outs[:count], outs[count:]

        def middle(small, step, layer, state, weight, returned):
            def body(gain_ref, router_ref, routes_ref, state_in, weight_in, returned_ref,
                     state_ref, slots_ref, weight_ref):
                state = combine(plan, state_in[...], weight_in[...], returned_ref[...])
                state_ref[...] = state
                emit_dispatch(
                    plan, state, gain_ref[layer : layer + 1], router_ref[layer],
                    routes_ref[step, layer], slots_ref, weight_ref,
                )

            return call(
                body, here(*small[2:], state, weight, returned), [state_shape, slots_shape, weight_shape]
            )

        def turn(small, state, weight, returned):
            def body(latent_ref, emb_ref, gain_ref, router_ref, routes_ref, state_in, weight_in, returned_ref,
                     first_ref, state_ref, slots_ref, weight_ref):
                state = combine(plan, state_in[...], weight_in[...], returned_ref[...])
                first = state - latent_ref[...]
                first_ref[...] = first
                moved = latent_ref[...] + step_size * first
                state = moved + (start_time + step_size) * emb_ref[...]
                state_ref[...] = state
                emit_dispatch(
                    plan, state, gain_ref[0:1], router_ref[0], routes_ref[1, 0], slots_ref, weight_ref
                )

            return call(
                body, here(*small, state, weight, returned),
                [state_shape, state_shape, slots_shape, weight_shape],
            )

        def finish(small, state, weight, returned, first):
            def body(latent_ref, state_in, weight_in, returned_ref, first_ref, next_ref, mean_ref):
                state = combine(plan, state_in[...], weight_in[...], returned_ref[...])
                first = first_ref[...]
                moved = latent_ref[...] + step_size * first
                mean = 0.5 * (first + (state - moved))
                mean_ref[...] = mean
                next_ref[...] = latent_ref[...] + step_size * mean

            return call(body, here(small[0], state, weight, returned, first), [out_shape, out_shape])

        each = plan.peers * CAP

        def compute(arrived, layer):
            def body(arrived_ref, up_ref, down_ref, out_ref):
                base = lax.axis_index("mp") * mine if plan.share > 1 else 0
                total = plan.rows * plan.peers

                def picks(shape, row_axis):
                    row = lax.broadcasted_iota(i32, shape, row_axis)
                    piece = lax.broadcasted_iota(i32, shape, 1 - row_axis)
                    local = div(row, each)
                    source = div(rem(row, each), CAP)
                    target = source * plan.block + local * CAP + rem(row, CAP)
                    return [
                        jnp.where(piece == target + p * plan.rows, 1.0, 0.0).astype(bf16)
                        for p in range(plan.parts)
                    ]

                arrived = arrived_ref[...]
                rows = jnp.concatenate(
                    [
                        jnp.dot(pick, arrived, preferred_element_type=f32).astype(bf16)
                        for pick in picks((total, plan.total), 0)
                    ],
                    axis=1,
                )
                results = []
                for local in range(mine):
                    hid = jax.nn.gelu(
                        lax.dot_general(
                            rows[local * each : (local + 1) * each],
                            up_ref[layer, base + local],
                            (((1,), (1,)), ((), ())),
                            preferred_element_type=f32,
                        ),
                        approximate=True,
                    ).astype(bf16)
                    results.append(
                        jnp.dot(hid, down_ref[layer, base + local], preferred_element_type=f32).astype(bf16)
                    )
                result = jnp.concatenate(results, axis=0)
                out = jnp.zeros((plan.total, plan.piece), f32)
                for p, pick in enumerate(picks((plan.total, total), 1)):
                    out = out + jnp.dot(
                        pick, result[:, p * plan.piece : (p + 1) * plan.piece], preferred_element_type=f32
                    )
                out_ref[...] = out.astype(bf16)

            return call(body, here(arrived, up_t, down_proj), [slots_shape], limit=6)[0]

        def exchange(x):
            return lax.all_to_all(x, plan.axes, split_axis=0, concat_axis=0, tiled=True)

        small, (state, slots, weight) = begin()
        for step in range(2):
            for layer in range(layers):
                returned = exchange(compute(exchange(slots), layer))
                if layer + 1 < layers:
                    state, slots, weight = middle(small, step, layer + 1, state, weight, returned)
                elif step == 0:
                    first, state, slots, weight = turn(small, state, weight, returned)
                else:
                    return tuple(finish(small, state, weight, returned, first))

    return run


def solution(mesh):
    placed = (
        P(("groups", "expert", "dp", "mp"), None),
        P(),
        P(),
        P(),
        P(None, "expert", None, "dp"),
        P(None, "expert", "dp", None),
        P(None, None, ("groups", "expert", "dp", "mp"), None),
    )
    return jax.shard_map(
        per_device_fn(mesh),
        mesh=mesh,
        in_specs=placed,
        out_specs=(
            P(("groups", "expert", "dp", "mp"), None),
            P(("groups", "expert", "dp", "mp"), None),
        ),
        check_vma=False,
    )
```

```python
import math

import jax
import jax.numpy as jnp
from jax import lax
from jax.experimental import pallas as pl
from jax.experimental.pallas import tpu as pltpu
from jax.sharding import PartitionSpec as P

CAP = 2

epsilon = 1e-06
start_time = 1.0
step_size = -0.5

bf16 = jnp.bfloat16
f32 = jnp.float32
i32 = jnp.int32


def div(x, n):
    if n & (n - 1) == 0:
        return x >> (n.bit_length() - 1)
    return x // n


def rem(x, n):
    if n & (n - 1) == 0:
        return x & (n - 1)
    return x - (x // n) * n


class Plan:
    def __init__(self, mesh, tokens, width, experts, local_experts):
        for shares in (("groups", "mp"), ("mp",), ()):
            share = math.prod(mesh.shape[axis] for axis in shares)
            if local_experts % share == 0:
                break
        self.shares = shares
        self.mine = local_experts // share
        self.axes = tuple(a for a in ("groups", "expert", "dp", "mp") if a in ("expert", "dp") + shares)
        self.sizes = [mesh.shape[axis] for axis in self.axes]
        self.peers = math.prod(self.sizes)
        self.tokens = tokens
        self.width = width
        self.experts = experts
        self.local_experts = local_experts
        self.rows = self.mine * CAP
        self.parts = 8 // math.gcd(8, self.rows)
        self.piece = width // self.parts
        self.block = self.rows * self.parts
        self.total = self.peers * self.block

    def first_expert(self, place):
        share = 0
        for axis in self.shares:
            size = self.sizes[self.axes.index(axis)]
            share = share * size + place[axis]
        return share * self.mine

    def where(self, index):
        peer = div(index, self.block)
        inner = rem(index, self.block)
        part = div(inner, self.rows)
        row = rem(inner, self.rows)
        place = {}
        for axis, size in reversed(list(zip(self.axes, self.sizes))):
            place[axis] = rem(peer, size)
            peer = div(peer, size)
        expert = place["expert"] * self.local_experts + self.first_expert(place)
        return part, expert + div(row, CAP), rem(row, CAP)


def column(row, tokens):
    eye = lax.broadcasted_iota(i32, (tokens, tokens), 0) == lax.broadcasted_iota(
        i32, (tokens, tokens), 1
    )
    return jnp.sum(jnp.where(eye, row, 0), axis=1, keepdims=True)


def by_part(plan, part, terms):
    return jnp.concatenate(
        [jnp.where(part == p, term, 0.0) for p in range(plan.parts) for term in terms], axis=0
    ).astype(bf16)


def combine(plan, state, weight, returned):
    part, _, _ = plan.where(lax.broadcasted_iota(i32, weight.shape, 1))
    high = weight.astype(bf16).astype(f32)
    middle = (weight - high).astype(bf16).astype(f32)
    low = weight - high - middle
    product = jnp.dot(
        by_part(plan, part, (high, middle, low)), returned, preferred_element_type=f32
    )
    t = plan.tokens
    pieces = []
    for p in range(plan.parts):
        base = 3 * t * p
        pieces.append(
            product[base : base + t]
            + product[base + t : base + 2 * t]
            + product[base + 2 * t : base + 3 * t]
        )
    return state + jnp.concatenate(pieces, axis=1)


def emit_dispatch(plan, state, gain, router, routes, slots_ref, weight_ref):
    t = plan.tokens
    first = column(routes[0:1], t)
    second = column(routes[1:2], t)
    part, expert, slot = plan.where(lax.broadcasted_iota(i32, (t, plan.total), 1))
    is_first = first == expert
    is_second = second == expert
    named = jnp.where(is_first | is_second, 1.0, 0.0)
    earlier = jnp.where(
        lax.broadcasted_iota(i32, (t, t), 1) < lax.broadcasted_iota(i32, (t, t), 0), 1.0, 0.0
    ).astype(bf16)
    before = jnp.dot(earlier, named.astype(bf16), preferred_element_type=f32)
    chosen = jnp.where(before == slot.astype(f32), named, 0.0)

    inverse = lax.rsqrt(jnp.mean(state * state, axis=1, keepdims=True) + epsilon)
    scaled = state * inverse * gain
    normed = scaled.astype(bf16)
    pieces = jnp.concatenate(
        [normed[:, p * plan.piece : (p + 1) * plan.piece] for p in range(plan.parts)], axis=0
    )
    slots_ref[...] = lax.dot_general(
        by_part(plan, part, (chosen,)), pieces, (((0,), (0,)), ((), ())), preferred_element_type=f32
    ).astype(bf16)
    logits = lax.dot_general(
        scaled,
        router,
        (((1,), (1,)), ((), ())),
        precision=lax.Precision.HIGHEST,
        preferred_element_type=f32,
    )
    lane = lax.broadcasted_iota(i32, (t, plan.experts), 1)
    gap = jnp.sum(
        jnp.where(lane == first, logits, 0.0) - jnp.where(lane == second, logits, 0.0),
        axis=1,
        keepdims=True,
    )
    mix = jax.nn.sigmoid(gap)
    weight_ref[...] = chosen * jnp.where(is_first, mix, 1.0 - mix)


def per_device_fn(mesh):
    vmem = pl.BlockSpec(memory_space=pltpu.VMEM)
    hbm = pl.BlockSpec(memory_space=pltpu.HBM)

    def call(body, args, outs, copies=0, limit=4):
        return pl.pallas_call(
            body,
            out_shape=outs,
            in_specs=[spec for spec, _ in args],
            out_specs=[vmem] * len(outs),
            scratch_shapes=[pltpu.SemaphoreType.DMA((copies,))] if copies else [],
            compiler_params=pltpu.CompilerParams(vmem_limit_bytes=limit << 20),
            cost_estimate=pl.CostEstimate(flops=10**11, transcendentals=0, bytes_accessed=10**9),
        )(*[arg for _, arg in args])

    def here(*arrays):
        return [(vmem, x) for x in arrays]

    def far(*arrays):
        return [(hbm, pltpu.with_memory_space_constraint(x, pltpu.HBM)) for x in arrays]

    def run(latent, time_embedding, norm_gain, router, up_proj, down_proj, routes):
        tokens, width = latent.shape
        layers, _, experts = router.shape
        local_experts = up_proj.shape[1]
        hidden = up_proj.shape[3]
        plan = Plan(mesh, tokens, width, experts, local_experts)
        mine = plan.mine

        embedding = time_embedding.reshape(1, width)
        router_t = jnp.swapaxes(router, 1, 2)
        routes_t = jnp.swapaxes(routes, 2, 3)
        up_t = jnp.swapaxes(up_proj, 2, 3)

        out_shape = jax.ShapeDtypeStruct((tokens, width), f32)
        state_shape = pltpu.VMEM((tokens, width), f32)
        slots_shape = pltpu.VMEM((plan.total, plan.piece), bf16)
        weight_shape = pltpu.VMEM((tokens, plan.total), f32)

        def begin():
            inputs = [latent, embedding, norm_gain, router_t, routes_t]
            count = len(inputs)

            def body(*refs):
                sources, copies = refs[:count], refs[count : 2 * count]
                state_ref, slots_ref, weight_ref, sems = refs[2 * count :]
                moves = [
                    pltpu.make_async_copy(source, target, sems.at[i])
                    for i, (source, target) in enumerate(zip(sources, copies))
                ]
                for move in moves:
                    move.start()
                for move in moves:
                    move.wait()
                latent_ref, emb_ref, gain_ref, router_ref, routes_ref = copies
                state = latent_ref[...] + start_time * emb_ref[...]
                state_ref[...] = state
                emit_dispatch(
                    plan, state, gain_ref[0:1], router_ref[0], routes_ref[0, 0], slots_ref, weight_ref
                )

            outs = call(
                body,
                far(*inputs),
                [pltpu.VMEM(x.shape, x.dtype) for x in inputs] + [state_shape, slots_shape, weight_shape],
                copies=count,
            )
            return outs[:count], outs[count:]

        def middle(small, step, layer, state, weight, returned):
            def body(gain_ref, router_ref, routes_ref, state_in, weight_in, returned_ref,
                     state_ref, slots_ref, weight_ref):
                state = combine(plan, state_in[...], weight_in[...], returned_ref[...])
                state_ref[...] = state
                emit_dispatch(
                    plan, state, gain_ref[layer : layer + 1], router_ref[layer],
                    routes_ref[step, layer], slots_ref, weight_ref,
                )

            return call(
                body, here(*small[2:], state, weight, returned), [state_shape, slots_shape, weight_shape]
            )

        def turn(small, state, weight, returned):
            def body(latent_ref, emb_ref, gain_ref, router_ref, routes_ref, state_in, weight_in, returned_ref,
                     first_ref, state_ref, slots_ref, weight_ref):
                state = combine(plan, state_in[...], weight_in[...], returned_ref[...])
                first = state - latent_ref[...]
                first_ref[...] = first
                moved = latent_ref[...] + step_size * first
                state = moved + (start_time + step_size) * emb_ref[...]
                state_ref[...] = state
                emit_dispatch(
                    plan, state, gain_ref[0:1], router_ref[0], routes_ref[1, 0], slots_ref, weight_ref
                )

            return call(
                body, here(*small, state, weight, returned),
                [state_shape, state_shape, slots_shape, weight_shape],
            )

        def finish(small, state, weight, returned, first):
            def body(latent_ref, state_in, weight_in, returned_ref, first_ref, next_ref, mean_ref):
                state = combine(plan, state_in[...], weight_in[...], returned_ref[...])
                first = first_ref[...]
                moved = latent_ref[...] + step_size * first
                mean = 0.5 * (first + (state - moved))
                mean_ref[...] = mean
                next_ref[...] = latent_ref[...] + step_size * mean

            return call(body, here(small[0], state, weight, returned, first), [out_shape, out_shape])

        each = plan.peers * CAP

        def compute(arrived, layer):
            def body(arrived_ref, up_ref, down_ref, out_ref):
                base = plan.first_expert({axis: lax.axis_index(axis) for axis in plan.shares})
                total = plan.rows * plan.peers

                def order(axis):
                    shape = (plan.total, plan.total)
                    row = lax.broadcasted_iota(i32, shape, axis)
                    piece = lax.broadcasted_iota(i32, shape, 1 - axis)
                    inner = rem(row, total)
                    source = div(rem(inner, each), CAP)
                    inside = div(row, total) * plan.rows + div(inner, each) * CAP + rem(row, CAP)
                    return jnp.where(piece == source * plan.block + inside, 1.0, 0.0).astype(bf16)

                ordered = jnp.dot(order(0), arrived_ref[...], preferred_element_type=f32).astype(bf16)
                rows = jnp.concatenate(
                    [ordered[p * total : (p + 1) * total] for p in range(plan.parts)], axis=1
                )
                hids = [
                    jax.nn.gelu(
                        lax.dot_general(
                            rows[local * each : (local + 1) * each],
                            up_ref[layer, base + local],
                            (((1,), (1,)), ((), ())),
                            preferred_element_type=f32,
                        ),
                        approximate=True,
                    ).astype(bf16)
                    for local in range(mine)
                ]
                result = jnp.concatenate(
                    [
                        jnp.dot(hids[local], down_ref[layer, base + local], preferred_element_type=f32).astype(
                            bf16
                        )
                        for local in range(mine)
                    ],
                    axis=0,
                )
                pieces = jnp.concatenate(
                    [result[:, p * plan.piece : (p + 1) * plan.piece] for p in range(plan.parts)], axis=0
                )
                out_ref[...] = jnp.dot(order(1), pieces, preferred_element_type=f32).astype(bf16)

            return call(body, here(arrived, up_t, down_proj), [slots_shape], limit=6)[0]

        def exchange(x):
            return lax.all_to_all(x, plan.axes, split_axis=0, concat_axis=0, tiled=True)

        small, (state, slots, weight) = begin()
        for step in range(2):
            for layer in range(layers):
                returned = exchange(compute(exchange(slots), layer))
                if layer + 1 < layers:
                    state, slots, weight = middle(small, step, layer + 1, state, weight, returned)
                elif step == 0:
                    first, state, slots, weight = turn(small, state, weight, returned)
                else:
                    return tuple(finish(small, state, weight, returned, first))

    return run


def solution(mesh):
    placed = (
        P(("groups", "expert", "dp", "mp"), None),
        P(),
        P(),
        P(),
        P(None, "expert", None, "dp"),
        P(None, "expert", "dp", None),
        P(None, None, ("groups", "expert", "dp", "mp"), None),
    )
    return jax.shard_map(
        per_device_fn(mesh),
        mesh=mesh,
        in_specs=placed,
        out_specs=(
            P(("groups", "expert", "dp", "mp"), None),
            P(("groups", "expert", "dp", "mp"), None),
        ),
        check_vma=False,
    )
```

```python
import math

import jax
import jax.numpy as jnp
from jax import lax
from jax.experimental import pallas as pl
from jax.experimental.pallas import tpu as pltpu
from jax.sharding import PartitionSpec as P

CAP = 2
TERMS = 2

epsilon = 1e-06
start_time = 1.0
step_size = -0.5

bf16 = jnp.bfloat16
f32 = jnp.float32
i32 = jnp.int32


def div(x, n):
    if n & (n - 1) == 0:
        return x >> (n.bit_length() - 1)
    return x // n


def rem(x, n):
    if n & (n - 1) == 0:
        return x & (n - 1)
    return x - (x // n) * n


class Plan:
    def __init__(self, mesh, tokens, width, experts, local_experts):
        for shares in (("groups", "mp"), ("mp",), ()):
            share = math.prod(mesh.shape[axis] for axis in shares)
            if local_experts % share == 0:
                break
        self.shares = shares
        self.mine = local_experts // share
        self.axes = tuple(a for a in ("groups", "expert", "dp", "mp") if a in ("expert", "dp") + shares)
        self.sizes = [mesh.shape[axis] for axis in self.axes]
        self.peers = math.prod(self.sizes)
        self.tokens = tokens
        self.width = width
        self.experts = experts
        self.local_experts = local_experts
        self.rows = self.mine * CAP
        self.parts = 8 // math.gcd(8, self.rows)
        self.piece = width // self.parts
        self.block = self.rows * self.parts
        self.total = self.peers * self.block

    def first_expert(self, place):
        share = 0
        for axis in self.shares:
            size = self.sizes[self.axes.index(axis)]
            share = share * size + place[axis]
        return share * self.mine

    def where(self, index):
        peer = div(index, self.block)
        inner = rem(index, self.block)
        part = div(inner, self.rows)
        row = rem(inner, self.rows)
        place = {}
        for axis, size in reversed(list(zip(self.axes, self.sizes))):
            place[axis] = rem(peer, size)
            peer = div(peer, size)
        expert = place["expert"] * self.local_experts + self.first_expert(place)
        return part, expert + div(row, CAP), rem(row, CAP)


def column(row, tokens):
    eye = lax.broadcasted_iota(i32, (tokens, tokens), 0) == lax.broadcasted_iota(
        i32, (tokens, tokens), 1
    )
    return jnp.sum(jnp.where(eye, row, 0), axis=1, keepdims=True)


def split(x, terms):
    out = []
    for _ in range(terms):
        out.append(x.astype(bf16))
        x = x - out[-1].astype(f32)
    return out


def by_part(plan, part, term):
    return [jnp.where(part == p, term, 0.0) for p in range(plan.parts)]


def select(plan, routes):
    t = plan.tokens
    first = column(routes[0:1], t)
    second = column(routes[1:2], t)
    part, expert, slot = plan.where(lax.broadcasted_iota(i32, (t, plan.total), 1))
    is_first = first == expert
    named = jnp.where(is_first | (second == expert), 1.0, 0.0)
    earlier = jnp.where(
        lax.broadcasted_iota(i32, (t, t), 1) < lax.broadcasted_iota(i32, (t, t), 0), 1.0, 0.0
    ).astype(bf16)
    before = jnp.dot(earlier, named.astype(bf16), preferred_element_type=f32)
    chosen = jnp.where(before == slot.astype(f32), named, 0.0)
    return first, second, part, is_first, chosen


def senders(plan, routes):
    _, _, part, _, chosen = select(plan, routes)
    return jnp.concatenate(by_part(plan, part, chosen), axis=0).T.astype(bf16)


def weights_of(plan, scaled, router, routes):
    first, second, part, is_first, chosen = select(plan, routes)
    product = lax.dot_general(
        jnp.concatenate(split(scaled, 3), axis=0),
        jnp.concatenate(split(router, 3), axis=0),
        (((1,), (1,)), ((), ())),
        preferred_element_type=f32,
    )
    t = plan.tokens
    logits = product[:t] + product[t : 2 * t] + product[2 * t :]
    lane = rem(lax.broadcasted_iota(i32, logits.shape, 1), plan.experts)
    gap = jnp.sum(
        jnp.where(lane == first, logits, 0.0) - jnp.where(lane == second, logits, 0.0),
        axis=1,
        keepdims=True,
    )
    mix = jax.nn.sigmoid(gap)
    weight = chosen * jnp.where(is_first, mix, 1.0 - mix)
    return jnp.concatenate(
        [term for piece in by_part(plan, part, weight) for term in split(piece, TERMS)], axis=0
    )


def combine(plan, state, weights, returned):
    product = jnp.dot(weights, returned, preferred_element_type=f32)
    t = plan.tokens
    pieces = []
    for p in range(plan.parts):
        piece = product[TERMS * t * p : TERMS * t * p + t]
        for term in range(1, TERMS):
            base = t * (TERMS * p + term)
            piece = piece + product[base : base + t]
        pieces.append(piece)
    return state + jnp.concatenate(pieces, axis=1)


def emit_dispatch(plan, state, gain, gather, scaled_ref, slots_ref):
    inverse = lax.rsqrt(jnp.mean(state * state, axis=1, keepdims=True) + epsilon)
    scaled = state * inverse * gain
    scaled_ref[...] = scaled
    normed = scaled.astype(bf16)
    pieces = jnp.concatenate(
        [normed[:, p * plan.piece : (p + 1) * plan.piece] for p in range(plan.parts)], axis=0
    )
    slots_ref[...] = jnp.dot(gather, pieces, preferred_element_type=f32).astype(bf16)


def per_device_fn(mesh):
    vmem = pl.BlockSpec(memory_space=pltpu.VMEM)
    hbm = pl.BlockSpec(memory_space=pltpu.HBM)

    def call(body, args, outs, copies=0, limit=4):
        return pl.pallas_call(
            body,
            out_shape=outs,
            in_specs=[spec for spec, _ in args],
            out_specs=[vmem] * len(outs),
            scratch_shapes=[pltpu.SemaphoreType.DMA((copies,))] if copies else [],
            compiler_params=pltpu.CompilerParams(vmem_limit_bytes=limit << 20),
            cost_estimate=pl.CostEstimate(flops=10**11, transcendentals=0, bytes_accessed=10**9),
        )(*[arg for _, arg in args])

    def here(*arrays):
        return [(vmem, x) for x in arrays]

    def far(*arrays):
        return [(hbm, pltpu.with_memory_space_constraint(x, pltpu.HBM)) for x in arrays]

    def run(latent, time_embedding, norm_gain, router, up_proj, down_proj, routes):
        tokens, width = latent.shape
        layers, _, experts = router.shape
        local_experts = up_proj.shape[1]
        hidden = up_proj.shape[3]
        plan = Plan(mesh, tokens, width, experts, local_experts)
        mine = plan.mine

        embedding = time_embedding.reshape(1, width)
        router_t = jnp.swapaxes(router, 1, 2)
        routes_t = jnp.swapaxes(routes, 2, 3)
        up_t = jnp.swapaxes(up_proj, 2, 3)

        out_shape = jax.ShapeDtypeStruct((tokens, width), f32)
        state_shape = pltpu.VMEM((tokens, width), f32)
        slots_shape = pltpu.VMEM((plan.total, plan.piece), bf16)
        gather_shape = pltpu.VMEM((plan.total, plan.parts * tokens), bf16)
        weight_shape = pltpu.VMEM((TERMS * plan.parts * tokens, plan.total), bf16)
        sent = [state_shape, state_shape, slots_shape]

        def begin():
            inputs = [latent, embedding, norm_gain, routes_t]
            count = len(inputs)

            def body(*refs):
                sources, copies = refs[:count], refs[count : 2 * count]
                state_ref, scaled_ref, slots_ref, sems = refs[2 * count :]
                moves = [
                    pltpu.make_async_copy(source, target, sems.at[i])
                    for i, (source, target) in enumerate(zip(sources, copies))
                ]
                for move in reversed(moves):
                    move.start()
                for move in reversed(moves):
                    move.wait()
                latent_ref, emb_ref, gain_ref, routes_ref = copies
                state = latent_ref[...] + start_time * emb_ref[...]
                state_ref[...] = state
                gather = senders(plan, routes_ref[0, 0])
                emit_dispatch(plan, state, gain_ref[0:1], gather, scaled_ref, slots_ref)

            outs = call(
                body,
                far(*inputs),
                [pltpu.VMEM(x.shape, x.dtype) for x in inputs] + sent,
                copies=count,
            )
            return outs[:count], outs[count:]

        def middle(gain, layer, state, weights, gather, returned):
            def body(gain_ref, state_in, weight_ref, gather_ref, returned_ref, state_ref, scaled_ref, slots_ref):
                state = combine(plan, state_in[...], weight_ref[...], returned_ref[...])
                state_ref[...] = state
                emit_dispatch(
                    plan, state, gain_ref[layer : layer + 1], gather_ref[...], scaled_ref, slots_ref
                )

            return call(body, here(gain, state, weights, gather, returned), sent)

        def turn(latent_s, emb, gain, state, weights, gather, returned):
            def body(latent_ref, emb_ref, gain_ref, state_in, weight_ref, gather_ref, returned_ref,
                     first_ref, state_ref, scaled_ref, slots_ref):
                state = combine(plan, state_in[...], weight_ref[...], returned_ref[...])
                first = state - latent_ref[...]
                first_ref[...] = first
                moved = latent_ref[...] + step_size * first
                state = moved + (start_time + step_size) * emb_ref[...]
                state_ref[...] = state
                emit_dispatch(plan, state, gain_ref[0:1], gather_ref[...], scaled_ref, slots_ref)

            return call(
                body, here(latent_s, emb, gain, state, weights, gather, returned), [state_shape] + sent
            )

        def finish(latent_s, state, weights, returned, first):
            def body(latent_ref, state_in, weight_ref, returned_ref, first_ref, next_ref, mean_ref):
                state = combine(plan, state_in[...], weight_ref[...], returned_ref[...])
                first = first_ref[...]
                moved = latent_ref[...] + step_size * first
                mean = 0.5 * (first + (state - moved))
                mean_ref[...] = mean
                next_ref[...] = latent_ref[...] + step_size * mean

            return call(body, here(latent_s, state, weights, returned, first), [out_shape, out_shape])

        each = plan.peers * CAP

        def compute(arrived, scaled, routes_s, step, layer):
            follows = step * layers + layer + 1
            last = follows == 2 * layers

            def body(arrived_ref, up_ref, down_ref, scaled_ref, router_ref, routes_ref,
                     out_ref, weight_ref, *gather_ref):
                base = plan.first_expert({axis: lax.axis_index(axis) for axis in plan.shares})
                total = plan.rows * plan.peers

                def order(axis):
                    shape = (plan.total, plan.total)
                    row = lax.broadcasted_iota(i32, shape, axis)
                    piece = lax.broadcasted_iota(i32, shape, 1 - axis)
                    inner = rem(row, total)
                    source = div(rem(inner, each), CAP)
                    inside = div(row, total) * plan.rows + div(inner, each) * CAP + rem(row, CAP)
                    return jnp.where(piece == source * plan.block + inside, 1.0, 0.0).astype(bf16)

                ordered = jnp.dot(order(0), arrived_ref[...], preferred_element_type=f32).astype(bf16)
                rows = jnp.concatenate(
                    [ordered[p * total : (p + 1) * total] for p in range(plan.parts)], axis=1
                )
                hids = [
                    jax.nn.gelu(
                        lax.dot_general(
                            rows[local * each : (local + 1) * each],
                            up_ref[layer, base + local],
                            (((1,), (1,)), ((), ())),
                            preferred_element_type=f32,
                        ),
                        approximate=True,
                    ).astype(bf16)
                    for local in range(mine)
                ]
                weight_ref[...] = weights_of(plan, scaled_ref[...], router_ref[layer], routes_ref[step, layer])
                if not last:
                    gather_ref[0][...] = senders(plan, routes_ref[follows // layers, follows % layers])
                result = jnp.concatenate(
                    [
                        jnp.dot(hids[local], down_ref[layer, base + local], preferred_element_type=f32).astype(
                            bf16
                        )
                        for local in range(mine)
                    ],
                    axis=0,
                )
                pieces = jnp.concatenate(
                    [result[:, p * plan.piece : (p + 1) * plan.piece] for p in range(plan.parts)], axis=0
                )
                out_ref[...] = jnp.dot(order(1), pieces, preferred_element_type=f32).astype(bf16)

            return call(
                body,
                here(arrived, up_t, down_proj, scaled, router_t, routes_s),
                [slots_shape, weight_shape] + [gather_shape] * (not last),
                limit=6,
            )

        def exchange(x):
            return lax.all_to_all(x, plan.axes, split_axis=0, concat_axis=0, tiled=True)

        (latent_s, emb, gain, routes_s), (state, scaled, slots) = begin()
        for step in range(2):
            for layer in range(layers):
                result, weights, *gather = compute(exchange(slots), scaled, routes_s, step, layer)
                returned = exchange(result)
                if layer + 1 < layers:
                    state, scaled, slots = middle(gain, layer + 1, state, weights, *gather, returned)
                elif step == 0:
                    first, state, scaled, slots = turn(
                        latent_s, emb, gain, state, weights, *gather, returned
                    )
                else:
                    return tuple(finish(latent_s, state, weights, returned, first))

    return run


def solution(mesh):
    placed = (
        P(("groups", "expert", "dp", "mp"), None),
        P(),
        P(),
        P(),
        P(None, "expert", None, "dp"),
        P(None, "expert", "dp", None),
        P(None, None, ("groups", "expert", "dp", "mp"), None),
    )
    return jax.shard_map(
        per_device_fn(mesh),
        mesh=mesh,
        in_specs=placed,
        out_specs=(
            P(("groups", "expert", "dp", "mp"), None),
            P(("groups", "expert", "dp", "mp"), None),
        ),
        check_vma=False,
    )
```

```python
import math

import jax
import jax.numpy as jnp
from jax import lax
from jax.experimental import pallas as pl
from jax.experimental.pallas import tpu as pltpu
from jax.sharding import PartitionSpec as P

CAP = 2
TERMS = 2

epsilon = 1e-06
start_time = 1.0
step_size = -0.5

bf16 = jnp.bfloat16
f32 = jnp.float32
i32 = jnp.int32


def div(x, n):
    if n & (n - 1) == 0:
        return x >> (n.bit_length() - 1)
    return x // n


def rem(x, n):
    if n & (n - 1) == 0:
        return x & (n - 1)
    return x - (x // n) * n


class Plan:
    def __init__(self, mesh, tokens, width, experts, local_experts):
        for shares in (("groups", "mp"), ("mp",), ()):
            share = math.prod(mesh.shape[axis] for axis in shares)
            if local_experts % share == 0:
                break
        self.shares = shares
        self.mine = local_experts // share
        self.axes = tuple(a for a in ("groups", "expert", "dp", "mp") if a in ("expert", "dp") + shares)
        self.sizes = [mesh.shape[axis] for axis in self.axes]
        self.peers = math.prod(self.sizes)
        self.tokens = tokens
        self.width = width
        self.experts = experts
        self.local_experts = local_experts
        self.rows = self.mine * CAP
        self.parts = 8 // math.gcd(8, self.rows)
        self.piece = width // self.parts
        self.block = self.rows * self.parts
        self.total = self.peers * self.block

    def first_expert(self, place):
        share = 0
        for axis in self.shares:
            size = self.sizes[self.axes.index(axis)]
            share = share * size + place[axis]
        return share * self.mine

    def where(self, index):
        peer = div(index, self.block)
        inner = rem(index, self.block)
        part = div(inner, self.rows)
        row = rem(inner, self.rows)
        place = {}
        for axis, size in reversed(list(zip(self.axes, self.sizes))):
            place[axis] = rem(peer, size)
            peer = div(peer, size)
        expert = place["expert"] * self.local_experts + self.first_expert(place)
        return part, expert + div(row, CAP), rem(row, CAP)


def column(row, tokens):
    eye = lax.broadcasted_iota(i32, (tokens, tokens), 0) == lax.broadcasted_iota(
        i32, (tokens, tokens), 1
    )
    return jnp.sum(jnp.where(eye, row, 0), axis=1, keepdims=True)


def split(x, terms):
    out = []
    for _ in range(terms):
        out.append(x.astype(bf16))
        x = x - out[-1].astype(f32)
    return out


def by_part(plan, part, term):
    return [jnp.where(part == p, term, 0.0) for p in range(plan.parts)]


def select(plan, routes):
    t = plan.tokens
    first = column(routes[0:1], t)
    second = column(routes[1:2], t)
    part, expert, slot = plan.where(lax.broadcasted_iota(i32, (t, plan.total), 1))
    is_first = first == expert
    named = jnp.where(is_first | (second == expert), 1.0, 0.0)
    earlier = jnp.where(
        lax.broadcasted_iota(i32, (t, t), 1) < lax.broadcasted_iota(i32, (t, t), 0), 1.0, 0.0
    ).astype(bf16)
    before = jnp.dot(earlier, named.astype(bf16), preferred_element_type=f32)
    chosen = jnp.where(before == slot.astype(f32), named, 0.0)
    return first, second, part, is_first, chosen


def senders(plan, routes):
    _, _, part, _, chosen = select(plan, routes)
    return jnp.concatenate(by_part(plan, part, chosen), axis=0).T.astype(bf16)


def weights_of(plan, scaled, router, routes):
    first, second, part, is_first, chosen = select(plan, routes)
    product = lax.dot_general(
        jnp.concatenate(split(scaled, 3), axis=0),
        jnp.concatenate(split(router, 3), axis=0),
        (((1,), (1,)), ((), ())),
        preferred_element_type=f32,
    )
    t = plan.tokens
    logits = product[:t] + product[t : 2 * t] + product[2 * t :]
    lane = rem(lax.broadcasted_iota(i32, logits.shape, 1), plan.experts)
    gap = jnp.sum(
        jnp.where(lane == first, logits, 0.0) - jnp.where(lane == second, logits, 0.0),
        axis=1,
        keepdims=True,
    )
    mix = jax.nn.sigmoid(gap)
    weight = chosen * jnp.where(is_first, mix, 1.0 - mix)
    return jnp.concatenate(
        [term for piece in by_part(plan, part, weight) for term in split(piece, TERMS)], axis=0
    )


def combine(plan, state, weights, returned):
    product = jnp.dot(weights, returned, preferred_element_type=f32)
    t = plan.tokens
    pieces = []
    for p in range(plan.parts):
        piece = product[TERMS * t * p : TERMS * t * p + t]
        for term in range(1, TERMS):
            base = t * (TERMS * p + term)
            piece = piece + product[base : base + t]
        pieces.append(piece)
    return state + jnp.concatenate(pieces, axis=1)


def emit_dispatch(plan, state, gain, gather, scaled_ref, slots_ref):
    inverse = lax.rsqrt(jnp.mean(state * state, axis=1, keepdims=True) + epsilon)
    scaled = state * inverse * gain
    scaled_ref[...] = scaled
    normed = scaled.astype(bf16)
    pieces = jnp.concatenate(
        [normed[:, p * plan.piece : (p + 1) * plan.piece] for p in range(plan.parts)], axis=0
    )
    slots_ref[...] = jnp.dot(gather, pieces, preferred_element_type=f32).astype(bf16)


def per_device_fn(mesh):
    vmem = pl.BlockSpec(memory_space=pltpu.VMEM)
    hbm = pl.BlockSpec(memory_space=pltpu.HBM)

    def call(body, args, outs, copies=0, limit=4, cost=10**11):
        return pl.pallas_call(
            body,
            out_shape=outs,
            in_specs=[spec for spec, _ in args],
            out_specs=[vmem] * len(outs),
            scratch_shapes=[pltpu.SemaphoreType.DMA((copies,))] if copies else [],
            compiler_params=pltpu.CompilerParams(vmem_limit_bytes=limit << 20),
            cost_estimate=pl.CostEstimate(flops=cost, transcendentals=0, bytes_accessed=0),
        )(*[arg for _, arg in args])

    def here(*arrays):
        return [(vmem, x) for x in arrays]

    def far(*arrays):
        return [(hbm, pltpu.with_memory_space_constraint(x, pltpu.HBM)) for x in arrays]

    def run(latent, time_embedding, norm_gain, router, up_proj, down_proj, routes):
        tokens, width = latent.shape
        layers, _, experts = router.shape
        local_experts = up_proj.shape[1]
        hidden = up_proj.shape[3]
        plan = Plan(mesh, tokens, width, experts, local_experts)
        mine = plan.mine

        embedding = time_embedding.reshape(1, width)
        router_t = jnp.swapaxes(router, 1, 2)
        routes_t = jnp.swapaxes(routes, 2, 3)
        up_t = jnp.swapaxes(up_proj, 2, 3)

        out_shape = jax.ShapeDtypeStruct((tokens, width), f32)
        state_shape = pltpu.VMEM((tokens, width), f32)
        slots_shape = pltpu.VMEM((plan.total, plan.piece), bf16)
        gather_shape = pltpu.VMEM((plan.total, plan.parts * tokens), bf16)
        weight_shape = pltpu.VMEM((TERMS * plan.parts * tokens, plan.total), bf16)
        sent = [state_shape, state_shape, slots_shape]

        def begin():
            inputs = [latent, embedding, norm_gain, routes_t]
            count = len(inputs)

            def body(*refs):
                sources, copies = refs[:count], refs[count : 2 * count]
                state_ref, scaled_ref, slots_ref, sems = refs[2 * count :]
                moves = [
                    pltpu.make_async_copy(source, target, sems.at[i])
                    for i, (source, target) in enumerate(zip(sources, copies))
                ]
                for move in reversed(moves):
                    move.start()
                for move in reversed(moves):
                    move.wait()
                latent_ref, emb_ref, gain_ref, routes_ref = copies
                state = latent_ref[...] + start_time * emb_ref[...]
                state_ref[...] = state
                gather = senders(plan, routes_ref[0, 0])
                emit_dispatch(plan, state, gain_ref[0:1], gather, scaled_ref, slots_ref)

            outs = call(
                body,
                far(*inputs),
                [pltpu.VMEM(x.shape, x.dtype) for x in inputs] + sent,
                copies=count,
            )
            return outs[:count], outs[count:]

        def middle(gain, layer, state, weights, gather, returned):
            def body(gain_ref, state_in, weight_ref, gather_ref, returned_ref, state_ref, scaled_ref, slots_ref):
                state = combine(plan, state_in[...], weight_ref[...], returned_ref[...])
                state_ref[...] = state
                emit_dispatch(
                    plan, state, gain_ref[layer : layer + 1], gather_ref[...], scaled_ref, slots_ref
                )

            return call(body, here(gain, state, weights, gather, returned), sent, cost=12300000000)

        def turn(latent_s, emb, gain, state, weights, gather, returned):
            def body(latent_ref, emb_ref, gain_ref, state_in, weight_ref, gather_ref, returned_ref,
                     first_ref, state_ref, scaled_ref, slots_ref):
                state = combine(plan, state_in[...], weight_ref[...], returned_ref[...])
                first = state - latent_ref[...]
                first_ref[...] = first
                moved = latent_ref[...] + step_size * first
                state = moved + (start_time + step_size) * emb_ref[...]
                state_ref[...] = state
                emit_dispatch(plan, state, gain_ref[0:1], gather_ref[...], scaled_ref, slots_ref)

            return call(
                body, here(latent_s, emb, gain, state, weights, gather, returned), [state_shape] + sent
            )

        def finish(latent_s, state, weights, returned, first):
            def body(latent_ref, state_in, weight_ref, returned_ref, first_ref, next_ref, mean_ref):
                state = combine(plan, state_in[...], weight_ref[...], returned_ref[...])
                first = first_ref[...]
                moved = latent_ref[...] + step_size * first
                mean = 0.5 * (first + (state - moved))
                mean_ref[...] = mean
                next_ref[...] = latent_ref[...] + step_size * mean

            return call(body, here(latent_s, state, weights, returned, first), [out_shape, out_shape])

        each = plan.peers * CAP

        def compute(arrived, scaled, routes_s, step, layer):
            follows = step * layers + layer + 1
            last = follows == 2 * layers

            def body(arrived_ref, up_ref, down_ref, scaled_ref, router_ref, routes_ref,
                     out_ref, weight_ref, *gather_ref):
                base = plan.first_expert({axis: lax.axis_index(axis) for axis in plan.shares})
                total = plan.rows * plan.peers

                def order(axis):
                    shape = (plan.total, plan.total)
                    row = lax.broadcasted_iota(i32, shape, axis)
                    piece = lax.broadcasted_iota(i32, shape, 1 - axis)
                    inner = rem(row, total)
                    source = div(rem(inner, each), CAP)
                    inside = div(row, total) * plan.rows + div(inner, each) * CAP + rem(row, CAP)
                    return jnp.where(piece == source * plan.block + inside, 1.0, 0.0).astype(bf16)

                ordered = jnp.dot(order(0), arrived_ref[...], preferred_element_type=f32).astype(bf16)
                rows = jnp.concatenate(
                    [ordered[p * total : (p + 1) * total] for p in range(plan.parts)], axis=1
                )
                hids = []
                for local in range(mine):
                    cuts = [0, -(-hidden // 256) * 128, hidden]
                    hids.append(jnp.concatenate([
                        jax.nn.gelu(
                            lax.dot_general(
                                rows[local * each : (local + 1) * each],
                                up_ref[layer, base + local, lo:hi],
                                (((1,), (1,)), ((), ())), preferred_element_type=f32,
                            ), approximate=True).astype(bf16)
                        for lo, hi in zip(cuts, cuts[1:])], axis=1))
                weight_ref[...] = weights_of(plan, scaled_ref[...], router_ref[layer], routes_ref[step, layer])
                if not last:
                    gather_ref[0][...] = senders(plan, routes_ref[follows // layers, follows % layers])
                result = jnp.concatenate(
                    [
                        jnp.dot(hids[local], down_ref[layer, base + local], preferred_element_type=f32).astype(
                            bf16
                        )
                        for local in range(mine)
                    ],
                    axis=0,
                )
                pieces = jnp.concatenate(
                    [result[:, p * plan.piece : (p + 1) * plan.piece] for p in range(plan.parts)], axis=0
                )
                out_ref[...] = jnp.dot(order(1), pieces, preferred_element_type=f32).astype(bf16)

            return call(
                body,
                here(arrived, up_t, down_proj, scaled, router_t, routes_s),
                [slots_shape, weight_shape] + [gather_shape] * (not last),
                limit=6,
            )

        def exchange(x):
            return lax.all_to_all(x, plan.axes, split_axis=0, concat_axis=0, tiled=True)

        (latent_s, emb, gain, routes_s), (state, scaled, slots) = begin()
        for step in range(2):
            for layer in range(layers):
                result, weights, *gather = compute(exchange(slots), scaled, routes_s, step, layer)
                returned = exchange(result)
                if layer + 1 < layers:
                    state, scaled, slots = middle(gain, layer + 1, state, weights, *gather, returned)
                elif step == 0:
                    first, state, scaled, slots = turn(
                        latent_s, emb, gain, state, weights, *gather, returned
                    )
                else:
                    return tuple(finish(latent_s, state, weights, returned, first))

    return run


def solution(mesh):
    placed = (
        P(("groups", "expert", "dp", "mp"), None),
        P(),
        P(),
        P(),
        P(None, "expert", None, "dp"),
        P(None, "expert", "dp", None),
        P(None, None, ("groups", "expert", "dp", "mp"), None),
    )
    return jax.shard_map(
        per_device_fn(mesh),
        mesh=mesh,
        in_specs=placed,
        out_specs=(
            P(("groups", "expert", "dp", "mp"), None),
            P(("groups", "expert", "dp", "mp"), None),
        ),
        check_vma=False,
    )
```
